32 devices in a mesh: outer: 4 (over x, core), rep: 2 (over y), fsdp: 4 (over z).
Axes of the slice: x: 2, y: 2, z: 4, core: 2. Of those that a mesh axis runs over, the one named last changes fastest.
Arguments:
- deltas: bfloat16 [8, 2304, 18432], P(('outer', 'rep'), None, 'fsdp'), may hold values from -0.119628906 to 0.119628906
- master: float32 [2304, 18432], P(('outer', 'rep'), 'fsdp'), may hold values from -0.125 to 0.125
- momentum: float32 [2304, 18432], P(('outer', 'rep'), 'fsdp'), may hold values from -0.06 to 0.06
- tokens: bfloat16 [8, 48, 2304], P(('outer', 'rep'), 'fsdp'), may hold values from -6 to 6
Outputs:
- new_master: float32 [2304, 18432], P(('outer', 'rep'), 'fsdp')
- hidden: bfloat16 [8, 48, 18432], P(('outer', 'rep'), None, 'fsdp')
The draws below stay inside these ranges and needn't reach their ends.
All inputs are finite; a program needn't handle non-finite values.
Results may differ from the reference program's by a relative error of at most 0.01.
Values may be sent and summed in bfloat16 or wider, within the bound.
A program may use at most 128 MiB of HBM per device.

```python
import jax
import jax.numpy as jnp
from jax import lax

D_WIN = 2304
FF_WIN = 18432
TOKENS = 48
REPLICAS = 8


def with_spikes(result, stream_key, source, target, parts, factor):
    def block_of(axis_at):
        return (jnp.arange(result.shape[axis_at]) // (result.shape[axis_at] // parts)).reshape((-1,) + (1,) * (result.ndim - 1 - axis_at))

    first = jax.random.permutation(stream_key, parts)[block_of(target)]
    other_side = (block_of(target) + parts // 2) % parts
    return jnp.where((block_of(source) == first) | (block_of(source) == other_side), factor * result, result)


def block_levels(rng, dims, cuts, low, high):
    level = 1.0
    for axis_at, blocks in cuts:
        draws = jax.random.uniform(jax.random.fold_in(jax.random.fold_in(rng, 6), axis_at), (blocks,), jnp.float32, low / len(cuts), high / len(cuts))
        level = level * jnp.repeat(jnp.exp(draws), dims[axis_at] // blocks).reshape((-1,) + (1,) * (len(dims) - 1 - axis_at))
    return level


def centred(key, shape, scale, reach, pieces=(), held_as=jnp.bfloat16):
    level = block_levels(key, shape, pieces, -0.22, 0.18) if pieces else 1.0
    array = jax.random.normal(key, shape, jnp.float32) * scale * level
    return jnp.minimum(jnp.maximum(array, -reach), reach).astype(held_as)


def gaussian_with(own_key, shape, width, limit, cuts, heavy, kind=jnp.bfloat16):
    result = width * jax.random.normal(own_key, shape, jnp.float32)
    if cuts:
        result = result * block_levels(own_key, shape, cuts, -0.22, 0.18)
    return jnp.clip(with_spikes(result, jax.random.fold_in(own_key, 3), *heavy), -limit, limit).astype(kind)


def setup_inputs(seed: int = 0) -> dict:
    keys = jax.random.split(jax.random.key(seed), 5)
    deltas = gaussian_with(keys[0], (REPLICAS, D_WIN, FF_WIN), 0.02, 0.119628906, ((0, 8), (2, 4)), (0, 1, 8, 2.0))
    master = centred(keys[1], (D_WIN, FF_WIN), D_WIN ** -0.5, 0.125, ((0, 8), (1, 4)), jnp.float32)
    momentum = centred(keys[2], (D_WIN, FF_WIN), 0.01, 0.06, ((0, 8), (1, 4)), jnp.float32)
    tokens = centred(keys[3], (REPLICAS, TOKENS, D_WIN), 1.0, 6.0, ((0, 8), (1, 4)))
    return dict(deltas=deltas, master=master, momentum=momentum, tokens=tokens)


outer_rate = 0.7
decay_rate = 0.9


def reference(deltas, master, momentum, tokens):
    def accumulate(total, delta):
        return total + delta.astype(jnp.float32), None

    summed, unused = lax.scan(accumulate, jnp.zeros(master.shape, jnp.float32), deltas)
    average = summed / deltas.shape[0]
    moment = decay_rate * momentum + average
    new_master = master - outer_rate * (average + decay_rate * moment)
    weights = new_master.astype(jnp.bfloat16)

    def forward(replica_tokens):
        product = jnp.dot(replica_tokens, weights, preferred_element_type=jnp.float32)
        return jax.nn.gelu(product, approximate=True).astype(jnp.bfloat16)

    hidden = lax.map(forward, tokens)
    return new_master, hidden
```

```python
import functools

import jax
import jax.numpy as jnp
from jax import lax
from jax.experimental import pallas as pl
from jax.experimental.pallas import tpu as pltpu
from jax.sharding import PartitionSpec as P

outer_rate = 0.7
decay_rate = 0.9
LANES = 128
PACK = 16
AHEAD = 4
MESH = pl.DeviceIdType.MESH


def plain_shards(deltas, master, momentum, tokens):
    outer_count = lax.axis_size("outer")
    rep_count = lax.axis_size("rep")
    terms = deltas[0].astype(jnp.float32)
    whole_tokens = lax.all_gather(tokens, "fsdp", axis=1, tiled=True)[0]
    summed = lax.psum_scatter(
        terms.astype(jnp.bfloat16), ("outer", "rep"), scatter_dimension=0, tiled=True
    ).astype(jnp.float32)
    average = summed / (outer_count * rep_count)
    moment = decay_rate * momentum + average
    new_master = master - outer_rate * (average + decay_rate * moment)
    weights = new_master.astype(jnp.bfloat16)
    product = jnp.dot(
        whole_tokens,
        lax.all_gather(weights, ("outer", "rep"), axis=0, tiled=True),
        preferred_element_type=jnp.float32,
    )
    hidden = jax.nn.gelu(product, approximate=True).astype(jnp.bfloat16)[None]
    return (new_master, hidden)


def f32(v):
    return v.astype(jnp.float32)


class Exchange:
    def __init__(self, given, held, r0, r1, r2, send, recv, at, peers):
        self.given, self.held = given, held
        self.r0, self.r1, self.r2 = r0, r1, r2
        self.send, self.recv = send, recv
        self.x, self.y = at
        self.core, self.peers = peers

    def copy(self, stage, src, dst, piece, peer):
        return pltpu.make_async_remote_copy(
            src_ref=src,
            dst_ref=dst.at[piece],
            send_sem=self.send.at[stage, piece],
            recv_sem=self.recv.at[stage, piece],
            device_id=peer,
            device_id_type=MESH,
        )

    def copy0(self, piece):
        return self.copy(0, self.given(piece), self.r0, piece, self.core)

    def copy1(self, piece, kind):
        if kind == 0:
            src = self.held.at[piece, 1 - self.x]
        else:
            src = self.held.at[piece, :, 1 - self.y]
        return self.copy(1, src, self.r1, piece, self.peers[kind])

    def spot2(self, kind):
        return (self.x, 1 - self.y) if kind == 0 else (1 - self.x, self.y)

    def copy2(self, piece, kind):
        a, b = self.spot2(kind)
        return self.copy(2, self.held.at[piece, a, b], self.r2, piece, self.peers[1 - kind])

    def go1(self, piece, kind):
        self.copy0(piece).wait_recv()
        for k in range(2):
            a, b = (1 - self.x, k) if kind == 0 else (k, 1 - self.y)
            total = f32(self.held[piece, a, b]) + f32(self.r0[piece, a, b])
            self.held[piece, a, b] = total.astype(jnp.bfloat16)
        self.copy1(piece, kind).start()

    def go2(self, piece, kind):
        self.copy1(piece, kind).wait_recv()
        a, b = self.spot2(kind)
        total = f32(self.held[piece, a, b]) + f32(self.r0[piece, a, b])
        total = total + f32(self.r1[piece, b if kind == 0 else a])
        self.held[piece, a, b] = total.astype(jnp.bfloat16)
        self.copy2(piece, kind).start()

    def last(self, piece, kind):
        self.copy2(piece, kind).wait_recv()
        total = f32(self.held[piece, self.x, self.y]) + f32(self.r0[piece, self.x, self.y])
        total = total + f32(self.r1[piece, self.y if kind == 0 else self.x])
        return total + f32(self.r2[piece])

    def sent(self, piece, kind):
        self.copy0(piece).wait_send()
        self.copy1(piece, kind).wait_send()
        self.copy2(piece, kind).wait_send()


def kernel(
    pieces, width, fsdp_count, count, token_rows,
    deltas, master, momentum, tokens, fresh_out, shown_out,
    held, d0, d1, d2, part, p0, p1, p2, mbuf, hbuf, vbuf, raw, cut, tokg, tokf, packed, tok,
    dsend, drecv, psend, precv, load_sem, state_sem,
    fsend, frecv, gsend, grecv, own_sem, fresh_sem, shown_sem,
):
    o, y, f = lax.axis_index("outer"), lax.axis_index("rep"), lax.axis_index("fsdp")
    x, c = o // 2, o % 2
    core_peer = {"outer": x * 2 + 1 - c}
    x_peer = {"outer": (1 - x) * 2 + c}
    y_peer = {"rep": 1 - y}

    def flip(v, bit):
        return 1 - v if bit else v

    others = [(dc, dx, dy) for dc in range(2) for dx in range(2) for dy in range(2)][1:]
    group = [
        ({"outer": flip(x, dx) * 2 + flip(c, dc), "rep": flip(y, dy)},
         (flip(x, dx) * 2 + flip(c, dc)) * 2 + flip(y, dy))
        for dc, dx, dy in others
    ]
    along = [{"fsdp": (f + k) % fsdp_count} for k in range(1, fsdp_count)]

    barrier = pltpu.get_barrier_semaphore()
    for peer in along + [g for g, _ in group]:
        pl.semaphore_signal(barrier, inc=1, device_id=peer, device_id_type=MESH)

    def columns(piece):
        return pl.ds(pl.multiple_of(piece * width, LANES), width)

    sums = Exchange(
        lambda piece: deltas.at[:, 1 - c, :, :, columns(piece)],
        held, d0, d1, d2, dsend, drecv, (x, y), (core_peer, (x_peer, y_peer)),
    )
    prods = Exchange(
        lambda piece: part.at[1 - c, piece],
        part.at[c], p0, p1, p2, psend, precv, (x, y), (core_peer, (x_peer, y_peer)),
    )

    def load(piece):
        return pltpu.make_async_copy(deltas.at[:, c, :, :, columns(piece)], held.at[piece], load_sem.at[piece])

    states = (
        pltpu.make_async_copy(master, mbuf, state_sem.at[0]),
        pltpu.make_async_copy(momentum, vbuf, state_sem.at[1]),
    )
    slot = (c * 2 + x) * 2 + y
    tok_load = pltpu.make_async_copy(tokens, raw, own_sem.at[2])
    tok_keep = pltpu.make_async_copy(cut.at[o * 2 + y], tokg.at[slot], own_sem.at[1])
    tok_group = [
        pltpu.make_async_remote_copy(
            src_ref=cut.at[share], dst_ref=tokg.at[slot], send_sem=gsend.at[k], recv_sem=grecv.at[k],
            device_id=peer, device_id_type=MESH,
        )
        for k, (peer, share) in enumerate(group)
    ]
    tok_own = pltpu.make_async_copy(tokg, tokf.at[f], own_sem.at[0])
    tok_along = [
        pltpu.make_async_remote_copy(
            src_ref=tokg, dst_ref=tokf.at[f], send_sem=fsend.at[k], recv_sem=frecv.at[k],
            device_id=peer, device_id_type=MESH,
        )
        for k, peer in enumerate(along)
    ]
    fresh_copy = pltpu.make_async_copy(mbuf, fresh_out, fresh_sem.at[0])

    def over(body):
        def step(i, carry):
            for kind in range(2):
                body(2 * i + kind, kind)
            return carry

        lax.fori_loop(0, pieces // 2, step, 0)

    def fetch(piece, kind):
        load(piece).start()

    def first(piece, kind):
        @pl.when(piece + AHEAD < pieces)
        def _():
            sums.copy0(piece + AHEAD).start()

        load(piece).wait()
        sums.go1(piece, kind)

    tok_load.start()
    over(fetch)
    pl.semaphore_wait(barrier, len(along) + len(group))
    for piece in range(min(AHEAD, pieces)):
        sums.copy0(piece).start()
    tok_load.wait()
    depth = cut.shape[2]
    cut[...] = jnp.zeros_like(cut)
    for g in range(count):
        cut[g, :token_rows] = f32(raw[...])[:, g * depth:(g + 1) * depth].astype(jnp.bfloat16)
    tok_keep.start()
    for copy in tok_group:
        copy.start()
    over(first)
    for copy in states:
        copy.start()
    tok_keep.wait()
    for copy in tok_group:
        copy.wait_recv()
    tok_own.start()
    for copy in tok_along:
        copy.start()
    tok_own.wait()
    for copy in tok_along:
        copy.wait_recv()
    for g in range(count):
        for k in range(fsdp_count):
            packed[g, pl.ds(k * token_rows, token_rows), :] = f32(tokf[k, g])[:token_rows]
    tok[...] = packed[...].astype(jnp.bfloat16).reshape(tok.shape)

    over(sums.go2)
    for copy in states:
        copy.wait()

    def update(piece, kind):
        at = columns(piece)
        average = sums.last(piece, kind) / count
        moment = decay_rate * vbuf[:, at] + average
        fresh = mbuf[:, at] - outer_rate * (average + decay_rate * moment)
        mbuf[:, at] = fresh
        product = jnp.dot(tok[...], fresh.astype(jnp.bfloat16), preferred_element_type=jnp.float32)
        product = product.astype(jnp.bfloat16).reshape((2, 2, 2) + hbuf.shape[:1] + (width,))
        part[0, piece] = product[0]
        part[1, piece] = product[1]
        prods.copy0(piece).start()

    def update_then(piece, kind):
        update(piece, kind)

        @pl.when(piece > 0)
        def _():
            prods.go1(piece - 1, 1 - kind)

    over(update_then)
    prods.go1(pieces - 1, 1)
    fresh_copy.start()
    over(prods.go2)

    def shown_copy(piece):
        return pltpu.make_async_copy(hbuf.at[:, columns(piece)], shown_out.at[:, columns(piece)], shown_sem.at[piece])

    def finish(piece, kind):
        v = prods.last(piece, kind)
        inner = 0.7978845608028654 * (v + 0.044715 * (v * v * v))
        hbuf[:, columns(piece)] = (0.5 * v * (1.0 + jnp.tanh(inner))).astype(jnp.bfloat16)
        shown_copy(piece).start()

    over(finish)

    def settle(piece, kind):
        sums.sent(piece, kind)
        prods.sent(piece, kind)
        shown_copy(piece).wait()

    over(settle)
    fresh_copy.wait()
    for copy in tok_along + tok_group:
        copy.wait_send()


def fast_shards(pieces, deltas, master, momentum, tokens):
    fsdp_count = lax.axis_size("fsdp")
    count = lax.axis_size("outer") * lax.axis_size("rep")
    depth, wide = deltas.shape[1:]
    rows = depth // count
    width = wide // pieces
    token_rows = tokens.shape[1]
    padded = -(-token_rows // PACK) * PACK
    own_tokens = token_rows * fsdp_count
    blocks = deltas.reshape(2, 2, 2, rows, wide)
    half = jnp.bfloat16
    dma = pltpu.SemaphoreType.DMA
    anywhere = pl.BlockSpec(memory_space=pl.ANY)
    new_master, hidden = pl.pallas_call(
        functools.partial(kernel, pieces, width, fsdp_count, count, token_rows),
        out_shape=(
            pltpu.VMEM((rows, wide), jnp.float32),
            pltpu.VMEM((own_tokens, wide), half),
        ),
        in_specs=[anywhere] * 4,
        out_specs=(anywhere, anywhere),
        scratch_shapes=[
            pltpu.VMEM((pieces, 2, 2, rows, width), half),
            pltpu.VMEM((pieces, 2, 2, rows, width), half),
            pltpu.VMEM((pieces, 2, rows, width), half),
            pltpu.VMEM((pieces, rows, width), half),
            pltpu.VMEM((2, pieces, 2, 2, own_tokens, width), half),
            pltpu.VMEM((pieces, 2, 2, own_tokens, width), half),
            pltpu.VMEM((pieces, 2, own_tokens, width), half),
            pltpu.VMEM((pieces, own_tokens, width), half),
            pltpu.VMEM((rows, wide), jnp.float32),
            pltpu.VMEM((own_tokens, wide), half),
            pltpu.VMEM((rows, wide), jnp.float32),
            pltpu.VMEM((token_rows, depth), half),
            pltpu.VMEM((count, padded, rows), half),
            pltpu.VMEM((count, padded, rows), half),
            pltpu.VMEM((fsdp_count, count, padded, rows), half),
            pltpu.VMEM((count, own_tokens, rows), jnp.float32),
            pltpu.VMEM((count * own_tokens, rows), half),
            dma((3, pieces)), dma((3, pieces)), dma((3, pieces)), dma((3, pieces)),
            dma((pieces,)), dma((2,)),
            dma((fsdp_count - 1,)), dma((fsdp_count - 1,)), dma((count - 1,)), dma((count - 1,)), dma((3,)),
            dma((1,)), dma((pieces,)),
        ],
        compiler_params=pltpu.CompilerParams(
            collective_id=0, has_side_effects=True, vmem_limit_bytes=58 * 1024 * 1024
        ),
    )(blocks, master, momentum, tokens[0])
    parts = 8 if rows % 64 == 0 else 4 if rows % 32 == 0 else 1
    return pl.pallas_call(
        functools.partial(write_out, parts),
        out_shape=(
            jax.ShapeDtypeStruct((rows, wide), jnp.float32),
            jax.ShapeDtypeStruct((1, own_tokens, wide), half),
        ),
        in_specs=[pl.BlockSpec(memory_space=pltpu.VMEM)] * 2,
        out_specs=(anywhere, anywhere),
        scratch_shapes=[dma((parts + 1,))],
        compiler_params=pltpu.CompilerParams(vmem_limit_bytes=1024 * 1024),
    )(
        pltpu.with_memory_space_constraint(new_master, pltpu.VMEM),
        pltpu.with_memory_space_constraint(hidden, pltpu.VMEM),
    )


def write_out(parts, fresh, shown, new_master, hidden, sem):
    rows = fresh.shape[0] // parts
    copies = [
        pltpu.make_async_copy(fresh.at[pl.ds(k * rows, rows)], new_master.at[pl.ds(k * rows, rows)], sem.at[k])
        for k in range(parts)
    ]
    copies.append(pltpu.make_async_copy(shown, hidden.at[0], sem.at[parts]))
    for copy in copies:
        copy.start()
    for copy in copies:
        copy.wait()


def pieces_for(mesh, deltas):
    if mesh.shape["outer"] != 4 or mesh.shape["rep"] != 2:
        return None
    count = mesh.shape["outer"] * mesh.shape["rep"]
    wide = deltas.shape[2] // mesh.shape["fsdp"]
    if deltas.shape[1] % (count * PACK):
        return None
    for pieces in (18, 16, 12, 10, 8, 6, 4, 2):
        if wide % (pieces * LANES) == 0:
            return pieces
    return None


def solution(mesh):
    in_specs = (
        P(("outer", "rep"), None, "fsdp"),
        P(("outer", "rep"), "fsdp"),
        P(("outer", "rep"), "fsdp"),
        P(("outer", "rep"), "fsdp", None),
    )
    out_specs = (P(("outer", "rep"), "fsdp"), P(("outer", "rep"), None, "fsdp"))

    def run(deltas, master, momentum, tokens):
        pieces = pieces_for(mesh, deltas)
        shards = plain_shards if pieces is None else functools.partial(fast_shards, pieces)
        return jax.shard_map(shards, mesh=mesh, in_specs=in_specs, out_specs=out_specs, check_vma=False)(
            deltas, master, momentum, tokens
        )

    return run
```

```python
import functools

import jax
import jax.numpy as jnp
from jax import lax
from jax.experimental import pallas as pl
from jax.experimental.pallas import tpu as pltpu
from jax.sharding import PartitionSpec as P

outer_rate = 0.7
decay_rate = 0.9
LANES = 128
PACK = 16
AHEAD = 2
MESH = pl.DeviceIdType.MESH


def plain_shards(deltas, master, momentum, tokens):
    outer_count = lax.axis_size("outer")
    rep_count = lax.axis_size("rep")
    terms = deltas[0].astype(jnp.float32)
    whole_tokens = lax.all_gather(tokens, "fsdp", axis=1, tiled=True)[0]
    summed = lax.psum_scatter(
        terms.astype(jnp.bfloat16), ("outer", "rep"), scatter_dimension=0, tiled=True
    ).astype(jnp.float32)
    average = summed / (outer_count * rep_count)
    moment = decay_rate * momentum + average
    new_master = master - outer_rate * (average + decay_rate * moment)
    weights = new_master.astype(jnp.bfloat16)
    product = jnp.dot(
        whole_tokens,
        lax.all_gather(weights, ("outer", "rep"), axis=0, tiled=True),
        preferred_element_type=jnp.float32,
    )
    hidden = jax.nn.gelu(product, approximate=True).astype(jnp.bfloat16)[None]
    return (new_master, hidden)


def f32(v):
    return v.astype(jnp.float32)


class Exchange:
    def __init__(self, given, held, r0, r1, r2, send, recv, at, peers):
        self.given, self.held = given, held
        self.r0, self.r1, self.r2 = r0, r1, r2
        self.send, self.recv = send, recv
        self.x, self.y = at
        self.core, self.peers = peers

    def copy(self, stage, src, dst, pair, peer):
        return pltpu.make_async_remote_copy(
            src_ref=src,
            dst_ref=dst,
            send_sem=self.send.at[stage],
            recv_sem=self.recv.at[stage, pair],
            device_id=peer,
            device_id_type=MESH,
        )

    def got(self, stage, pair):
        box = (self.r0, self.r1, self.r2)[stage].at[pl.ds(2 * pair, 2)]
        self.copy(stage, box, box, pair, self.core).wait_recv()

    def sent(self):
        for stage, box in enumerate((self.r0, self.r1, self.r2)):
            self.copy(stage, box, box, 0, self.core).wait_send()

    def spot2(self, kind):
        return (self.x, 1 - self.y) if kind == 0 else (1 - self.x, self.y)

    def go0(self, pair):
        for kind in range(2):
            piece = 2 * pair + kind
            self.copy(0, self.given(piece), self.r0.at[piece], pair, self.core).start()

    def go1(self, pair):
        self.got(0, pair)
        for kind in range(2):
            piece = 2 * pair + kind
            for k in range(2):
                a, b = (1 - self.x, k) if kind == 0 else (k, 1 - self.y)
                total = f32(self.held[piece, a, b]) + f32(self.r0[piece, a, b])
                self.held[piece, a, b] = total.astype(jnp.bfloat16)
            src = self.held.at[piece, 1 - self.x] if kind == 0 else self.held.at[piece, :, 1 - self.y]
            self.copy(1, src, self.r1.at[piece], pair, self.peers[kind]).start()

    def go2(self, pair):
        self.got(1, pair)
        for kind in range(2):
            piece = 2 * pair + kind
            a, b = self.spot2(kind)
            total = f32(self.held[piece, a, b]) + f32(self.r0[piece, a, b])
            total = total + f32(self.r1[piece, b if kind == 0 else a])
            self.held[piece, a, b] = total.astype(jnp.bfloat16)
            self.copy(2, self.held.at[piece, a, b], self.r2.at[piece], pair, self.peers[1 - kind]).start()

    def last(self, piece, kind):
        total = f32(self.held[piece, self.x, self.y]) + f32(self.r0[piece, self.x, self.y])
        total = total + f32(self.r1[piece, self.y if kind == 0 else self.x])
        return total + f32(self.r2[piece])


def kernel(
    pieces, width, fsdp_count, count, token_rows,
    deltas, master, momentum, tokens, fresh_out, shown_out,
    held, d0, d1, d2, part, p0, p1, p2, mbuf, hbuf, vbuf, raw, cut, tokg, tokf, packed, tok,
    dsend, drecv, psend, precv, load_sem, state_sem,
    fsend, frecv, gsend, grecv, own_sem, fresh_sem, shown_sem,
    core_sem, plane_sem, all_sem,
):
    o, y, f = lax.axis_index("outer"), lax.axis_index("rep"), lax.axis_index("fsdp")
    x, c = o // 2, o % 2
    core_peer = {"outer": x * 2 + 1 - c}
    x_peer = {"outer": (1 - x) * 2 + c}
    y_peer = {"rep": 1 - y}

    def flip(v, bit):
        return 1 - v if bit else v

    others = [(dc, dx, dy) for dc in range(2) for dx in range(2) for dy in range(2)][1:]
    group = [
        ({"outer": flip(x, dx) * 2 + flip(c, dc), "rep": flip(y, dy)},
         (flip(x, dx) * 2 + flip(c, dc)) * 2 + flip(y, dy))
        for dc, dx, dy in others
    ]
    along = [{"fsdp": (f + k) % fsdp_count} for k in range(1, fsdp_count)]

    corner = x * y
    lead = corner * c

    def counter(at_x, at_y):
        return {"outer": at_x * 2 + 1 - at_x * at_y, "rep": at_y}

    barrier = pltpu.get_barrier_semaphore()
    for at_x, at_y in ((1 - x, y), (x, 1 - y), (1 - x, 1 - y)):
        pl.semaphore_signal(barrier, inc=1, device_id=counter(at_x, at_y), device_id_type=MESH)

    @pl.when(c == 1)
    def _():
        pl.semaphore_signal(barrier, inc=1, device_id=core_peer, device_id_type=MESH)

    def columns(piece):
        return pl.ds(pl.multiple_of(piece * width, LANES), width)

    sums = Exchange(
        lambda piece: deltas.at[:, 1 - c, :, :, columns(piece)],
        held, d0, d1, d2, dsend, drecv, (x, y), (core_peer, (x_peer, y_peer)),
    )
    prods = Exchange(
        lambda piece: part.at[1 - c, piece],
        part.at[c], p0, p1, p2, psend, precv, (x, y), (core_peer, (x_peer, y_peer)),
    )

    def load(pair, kind):
        piece = 2 * pair + kind
        return pltpu.make_async_copy(deltas.at[:, c, :, :, columns(piece)], held.at[piece], load_sem.at[piece])

    states = (
        pltpu.make_async_copy(master, mbuf, state_sem.at[0]),
        pltpu.make_async_copy(momentum, vbuf, state_sem.at[1]),
    )
    slot = (c * 2 + x) * 2 + y
    tok_load = pltpu.make_async_copy(tokens, raw, own_sem.at[2])
    tok_keep = pltpu.make_async_copy(cut.at[o * 2 + y], tokg.at[slot], own_sem.at[1])
    tok_group = [
        pltpu.make_async_remote_copy(
            src_ref=cut.at[share], dst_ref=tokg.at[slot], send_sem=gsend.at[0], recv_sem=grecv.at[0],
            device_id=peer, device_id_type=MESH,
        )
        for peer, share in group
    ]
    group_all = pltpu.make_async_remote_copy(
        src_ref=cut.at[pl.ds(0, count - 1)], dst_ref=tokg.at[pl.ds(0, count - 1)], send_sem=gsend.at[0],
        recv_sem=grecv.at[0], device_id=core_peer, device_id_type=MESH,
    )
    tok_own = pltpu.make_async_copy(tokg, tokf.at[f], own_sem.at[0])
    tok_along = [
        pltpu.make_async_remote_copy(
            src_ref=tokg, dst_ref=tokf.at[f], send_sem=fsend.at[0], recv_sem=frecv.at[0],
            device_id=peer, device_id_type=MESH,
        )
        for peer in along
    ]
    along_box = tokf.at[pl.ds(0, fsdp_count - 1)]
    along_all = pltpu.make_async_remote_copy(
        src_ref=along_box, dst_ref=along_box, send_sem=fsend.at[0], recv_sem=frecv.at[0],
        device_id=core_peer, device_id_type=MESH,
    )
    fresh_copy = pltpu.make_async_copy(mbuf, fresh_out, fresh_sem.at[0])

    pairs = pieces // 2

    def over(body):
        def step(pair, carry):
            body(pair)
            return carry

        lax.fori_loop(0, pairs, step, 0)

    def fetch(pair):
        @pl.when(pair > 0)
        def _():
            for kind in range(2):
                load(pair, kind).start()

    def first(pair):
        @pl.when(pair + AHEAD < pairs)
        def _():
            sums.go0(pair + AHEAD)

        for kind in range(2):
            load(pair, kind).wait()
        sums.go1(pair)

    tok_load.start()
    for kind in range(2):
        load(0, kind).start()

    @pl.when(c == 0)
    def _():
        pl.semaphore_wait(barrier, 1 + 6 * corner)
        pl.semaphore_signal(core_sem, inc=1, device_id=core_peer, device_id_type=MESH)

    @pl.when(c == 1)
    def _():
        pl.semaphore_wait(core_sem, 1)

    for pair in range(min(AHEAD, pairs)):
        sums.go0(pair)
    over(fetch)

    @pl.when(lead == 1)
    def _():
        for peer in along:
            pl.semaphore_signal(barrier, inc=1, device_id=peer, device_id_type=MESH)

    tok_load.wait()
    depth = cut.shape[2]
    cut[...] = jnp.zeros_like(cut)
    for g in range(count):
        cut[g, :token_rows] = f32(raw[...])[:, g * depth:(g + 1) * depth].astype(jnp.bfloat16)
    tok_keep.start()

    @pl.when((c == 1) & (corner == 0))
    def _():
        pl.semaphore_wait(barrier, 6)
        pl.semaphore_signal(plane_sem, inc=1, device_id=core_peer, device_id_type=MESH)

    @pl.when((c == 0) & (corner == 0))
    def _():
        pl.semaphore_wait(plane_sem, 1)

    for copy in tok_group:
        copy.start()
    over(first)
    for copy in states:
        copy.start()
    tok_keep.wait()
    group_all.wait_recv()
    tok_own.start()

    @pl.when(lead == 1)
    def _():
        pl.semaphore_wait(barrier, len(along))
        for peer, _ in group:
            pl.semaphore_signal(all_sem, inc=1, device_id=peer, device_id_type=MESH)

    @pl.when(lead == 0)
    def _():
        pl.semaphore_wait(all_sem, 1)

    for copy in tok_along:
        copy.start()
    tok_own.wait()
    along_all.wait_recv()
    for g in range(count):
        for k in range(fsdp_count):
            packed[g, pl.ds(k * token_rows, token_rows), :] = f32(tokf[k, g])[:token_rows]
    tok[...] = packed[...].astype(jnp.bfloat16).reshape(tok.shape)

    over(sums.go2)
    for copy in states:
        copy.wait()

    def update(pair):
        sums.got(2, pair)
        for kind in range(2):
            piece = 2 * pair + kind
            at = columns(piece)
            average = sums.last(piece, kind) / count
            moment = decay_rate * vbuf[:, at] + average
            fresh = mbuf[:, at] - outer_rate * (average + decay_rate * moment)
            mbuf[:, at] = fresh
            product = jnp.dot(tok[...], fresh.astype(jnp.bfloat16), preferred_element_type=jnp.float32)
            product = product.astype(jnp.bfloat16).reshape((2, 2, 2) + hbuf.shape[:1] + (width,))
            part[0, piece] = product[0]
            part[1, piece] = product[1]
        prods.go0(pair)

        @pl.when(pair > 0)
        def _():
            prods.go1(pair - 1)

    over(update)
    prods.go1(pairs - 1)
    fresh_copy.start()
    over(prods.go2)

    def shown_copy(pair):
        at = pl.ds(pl.multiple_of(pair * 2 * width, LANES), 2 * width)
        return pltpu.make_async_copy(hbuf.at[:, at], shown_out.at[:, at], shown_sem.at[0])

    def finish(pair):
        prods.got(2, pair)
        for kind in range(2):
            piece = 2 * pair + kind
            v = prods.last(piece, kind)
            inner = 0.7978845608028654 * (v + 0.044715 * (v * v * v))
            hbuf[:, columns(piece)] = (0.5 * v * (1.0 + jnp.tanh(inner))).astype(jnp.bfloat16)
        shown_copy(pair).start()

    over(finish)
    sums.sent()
    prods.sent()
    group_all.wait_send()
    along_all.wait_send()
    fresh_copy.wait()
    pltpu.make_async_copy(hbuf, shown_out, shown_sem.at[0]).wait()


def fast_shards(pieces, deltas, master, momentum, tokens):
    fsdp_count = lax.axis_size("fsdp")
    count = lax.axis_size("outer") * lax.axis_size("rep")
    depth, wide = deltas.shape[1:]
    rows = depth // count
    width = wide // pieces
    token_rows = tokens.shape[1]
    padded = -(-token_rows // PACK) * PACK
    own_tokens = token_rows * fsdp_count
    blocks = deltas.reshape(2, 2, 2, rows, wide)
    half = jnp.bfloat16
    dma = pltpu.SemaphoreType.DMA
    regular = pltpu.SemaphoreType.REGULAR
    anywhere = pl.BlockSpec(memory_space=pl.ANY)
    new_master, hidden = pl.pallas_call(
        functools.partial(kernel, pieces, width, fsdp_count, count, token_rows),
        out_shape=(
            pltpu.VMEM((rows, wide), jnp.float32),
            pltpu.VMEM((own_tokens, wide), half),
        ),
        in_specs=[anywhere] * 4,
        out_specs=(anywhere, anywhere),
        scratch_shapes=[
            pltpu.VMEM((pieces, 2, 2, rows, width), half),
            pltpu.VMEM((pieces, 2, 2, rows, width), half),
            pltpu.VMEM((pieces, 2, rows, width), half),
            pltpu.VMEM((pieces, rows, width), half),
            pltpu.VMEM((2, pieces, 2, 2, own_tokens, width), half),
            pltpu.VMEM((pieces, 2, 2, own_tokens, width), half),
            pltpu.VMEM((pieces, 2, own_tokens, width), half),
            pltpu.VMEM((pieces, own_tokens, width), half),
            pltpu.VMEM((rows, wide), jnp.float32),
            pltpu.VMEM((own_tokens, wide), half),
            pltpu.VMEM((rows, wide), jnp.float32),
            pltpu.VMEM((token_rows, depth), half),
            pltpu.VMEM((count, padded, rows), half),
            pltpu.VMEM((count, padded, rows), half),
            pltpu.VMEM((fsdp_count, count, padded, rows), half),
            pltpu.VMEM((count, own_tokens, rows), jnp.float32),
            pltpu.VMEM((count * own_tokens, rows), half),
            dma((3,)), dma((3, pieces // 2)), dma((3,)), dma((3, pieces // 2)),
            dma((pieces,)), dma((2,)),
            dma((1,)), dma((1,)), dma((1,)), dma((1,)), dma((3,)),
            dma((1,)), dma((1,)),
            regular, regular, regular,
        ],
        compiler_params=pltpu.CompilerParams(
            collective_id=0, has_side_effects=True, vmem_limit_bytes=58 * 1024 * 1024
        ),
    )(blocks, master, momentum, tokens[0])
    parts = 8 if rows % 64 == 0 else 4 if rows % 32 == 0 else 1
    return pl.pallas_call(
        functools.partial(write_out, parts),
        out_shape=(
            jax.ShapeDtypeStruct((rows, wide), jnp.float32),
            jax.ShapeDtypeStruct((1, own_tokens, wide), half),
        ),
        in_specs=[pl.BlockSpec(memory_space=pltpu.VMEM)] * 2,
        out_specs=(anywhere, anywhere),
        scratch_shapes=[dma((parts + 1,))],
        compiler_params=pltpu.CompilerParams(vmem_limit_bytes=1024 * 1024),
    )(
        pltpu.with_memory_space_constraint(new_master, pltpu.VMEM),
        pltpu.with_memory_space_constraint(hidden, pltpu.VMEM),
    )


def write_out(parts, fresh, shown, new_master, hidden, sem):
    rows = fresh.shape[0] // parts
    copies = [
        pltpu.make_async_copy(fresh.at[pl.ds(k * rows, rows)], new_master.at[pl.ds(k * rows, rows)], sem.at[k])
        for k in range(parts)
    ]
    copies.append(pltpu.make_async_copy(shown, hidden.at[0], sem.at[parts]))
    for copy in copies:
        copy.start()
    for copy in copies:
        copy.wait()


def pieces_for(mesh, deltas):
    if mesh.shape["outer"] != 4 or mesh.shape["rep"] != 2:
        return None
    count = mesh.shape["outer"] * mesh.shape["rep"]
    wide = deltas.shape[2] // mesh.shape["fsdp"]
    if deltas.shape[1] % (count * PACK):
        return None
    for pieces in (18, 16, 12, 10, 8, 6, 4, 2):
        if wide % (pieces * LANES) == 0:
            return pieces
    return None


def solution(mesh):
    in_specs = (
        P(("outer", "rep"), None, "fsdp"),
        P(("outer", "rep"), "fsdp"),
        P(("outer", "rep"), "fsdp"),
        P(("outer", "rep"), "fsdp", None),
    )
    out_specs = (P(("outer", "rep"), "fsdp"), P(("outer", "rep"), None, "fsdp"))

    def run(deltas, master, momentum, tokens):
        pieces = pieces_for(mesh, deltas)
        shards = plain_shards if pieces is None else functools.partial(fast_shards, pieces)
        return jax.shard_map(shards, mesh=mesh, in_specs=in_specs, out_specs=out_specs, check_vma=False)(
            deltas, master, momentum, tokens
        )

    return run
```

```python
import functools

import jax
import jax.numpy as jnp
from jax import lax
from jax.experimental import pallas as pl
from jax.experimental.pallas import tpu as pltpu
from jax.sharding import PartitionSpec as P

outer_rate = 0.7
decay_rate = 0.9
LANES = 128
PACK = 16
AHEAD = 2
HEAD = 3
LAG = 2
MESH = pl.DeviceIdType.MESH


def plain_shards(deltas, master, momentum, tokens):
    outer_count = lax.axis_size("outer")
    rep_count = lax.axis_size("rep")
    terms = deltas[0].astype(jnp.float32)
    whole_tokens = lax.all_gather(tokens, "fsdp", axis=1, tiled=True)[0]
    summed = lax.psum_scatter(
        terms.astype(jnp.bfloat16), ("outer", "rep"), scatter_dimension=0, tiled=True
    ).astype(jnp.float32)
    average = summed / (outer_count * rep_count)
    moment = decay_rate * momentum + average
    new_master = master - outer_rate * (average + decay_rate * moment)
    weights = new_master.astype(jnp.bfloat16)
    product = jnp.dot(
        whole_tokens,
        lax.all_gather(weights, ("outer", "rep"), axis=0, tiled=True),
        preferred_element_type=jnp.float32,
    )
    hidden = jax.nn.gelu(product, approximate=True).astype(jnp.bfloat16)[None]
    return (new_master, hidden)


def f32(v):
    return v.astype(jnp.float32)


class Exchange:
    def __init__(self, given, held, r0, r1, r2, send, recv, at, peers):
        self.given, self.held = given, held
        self.r0, self.r1, self.r2 = r0, r1, r2
        self.send, self.recv = send, recv
        self.x, self.y = at
        self.core, self.peers = peers

    def copy(self, stage, src, dst, pair, peer):
        return pltpu.make_async_remote_copy(
            src_ref=src,
            dst_ref=dst,
            send_sem=self.send.at[stage],
            recv_sem=self.recv.at[stage, pair],
            device_id=peer,
            device_id_type=MESH,
        )

    def got(self, stage, pair):
        box = (self.r0, self.r1, self.r2)[stage].at[pl.ds(2 * pair, 2)]
        self.copy(stage, box, box, pair, self.core).wait_recv()

    def sent(self):
        for stage, box in enumerate((self.r0, self.r1, self.r2)):
            self.copy(stage, box, box, 0, self.core).wait_send()

    def spot2(self, kind):
        return (self.x, 1 - self.y) if kind == 0 else (1 - self.x, self.y)

    def go0(self, pair):
        for kind in range(2):
            piece = 2 * pair + kind
            self.copy(0, self.given(piece), self.r0.at[piece], pair, self.core).start()

    def forward1(self, pair, at):
        for kind in range(2):
            piece = 2 * pair + kind
            for k in range(2):
                a, b = (1 - self.x, k) if kind == 0 else (k, 1 - self.y)
                total = f32(self.held[piece, a, b, at]) + f32(self.r0[piece, a, b, at])
                self.held[piece, a, b, at] = total.astype(jnp.bfloat16)
            src = self.held.at[piece, 1 - self.x, :, at] if kind == 0 else self.held.at[piece, :, 1 - self.y, at]
            self.copy(1, src, self.r1.at[piece, :, at], pair, self.peers[kind]).start()

    def go1(self, pair):
        self.got(0, pair)
        self.forward1(pair, pl.ds(0, self.r0.shape[3]))

    def head0(self, cuts, sem):
        for h, at in enumerate(cuts):
            for kind in range(2):
                pltpu.make_async_remote_copy(
                    src_ref=self.given(kind).at[:, :, at], dst_ref=self.r0.at[kind, :, :, at],
                    send_sem=self.send.at[0], recv_sem=sem.at[h], device_id=self.core, device_id_type=MESH,
                ).start()

    def head1(self, cuts, sem):
        for h, at in enumerate(cuts):
            box = self.r0.at[pl.ds(0, 2), :, :, at]
            pltpu.make_async_remote_copy(
                src_ref=box, dst_ref=box, send_sem=self.send.at[0], recv_sem=sem.at[h],
                device_id=self.core, device_id_type=MESH,
            ).wait_recv()
            self.forward1(0, at)

    def go2(self, pair):
        self.got(1, pair)
        for kind in range(2):
            piece = 2 * pair + kind
            a, b = self.spot2(kind)
            total = f32(self.held[piece, a, b]) + f32(self.r0[piece, a, b])
            total = total + f32(self.r1[piece, b if kind == 0 else a])
            self.held[piece, a, b] = total.astype(jnp.bfloat16)
            self.copy(2, self.held.at[piece, a, b], self.r2.at[piece], pair, self.peers[1 - kind]).start()

    def last(self, piece, kind):
        total = f32(self.held[piece, self.x, self.y]) + f32(self.r0[piece, self.x, self.y])
        total = total + f32(self.r1[piece, self.y if kind == 0 else self.x])
        return total + f32(self.r2[piece])


def kernel(
    pieces, width, fsdp_count, count, token_rows,
    deltas, master, momentum, tokens, fresh_out, shown_out,
    held, d0, d1, d2, part, p0, p1, p2, mbuf, hbuf, vbuf, raw, cut, tokg, tokf, packed, tok,
    dsend, drecv, psend, precv, load_sem, state_sem, head_sem,
    fsend, frecv, gsend, grecv, own_sem, fresh_sem, shown_sem,
    core_sem, plane_sem, all_sem,
):
    o, y, f = lax.axis_index("outer"), lax.axis_index("rep"), lax.axis_index("fsdp")
    x, c = o // 2, o % 2
    core_peer = {"outer": x * 2 + 1 - c}
    x_peer = {"outer": (1 - x) * 2 + c}
    y_peer = {"rep": 1 - y}

    def flip(v, bit):
        return 1 - v if bit else v

    others = [(dc, dx, dy) for dc in range(2) for dx in range(2) for dy in range(2)][1:]
    group = [
        ({"outer": flip(x, dx) * 2 + flip(c, dc), "rep": flip(y, dy)},
         (flip(x, dx) * 2 + flip(c, dc)) * 2 + flip(y, dy))
        for dc, dx, dy in others
    ]
    along = [{"fsdp": (f + k) % fsdp_count} for k in range(1, fsdp_count)]

    corner = x * y
    lead = corner * c

    def counter(at_x, at_y):
        return {"outer": at_x * 2 + 1 - at_x * at_y, "rep": at_y}

    barrier = pltpu.get_barrier_semaphore()
    for at_x, at_y in ((1 - x, y), (x, 1 - y), (1 - x, 1 - y)):
        pl.semaphore_signal(barrier, inc=1, device_id=counter(at_x, at_y), device_id_type=MESH)

    @pl.when(c == 1)
    def _():
        pl.semaphore_signal(barrier, inc=1, device_id=core_peer, device_id_type=MESH)

    def columns(piece):
        return pl.ds(pl.multiple_of(piece * width, LANES), width)

    sums = Exchange(
        lambda piece: deltas.at[:, 1 - c, :, :, columns(piece)],
        held, d0, d1, d2, dsend, drecv, (x, y), (core_peer, (x_peer, y_peer)),
    )
    prods = Exchange(
        lambda piece: part.at[1 - c, piece],
        part.at[c], p0, p1, p2, psend, precv, (x, y), (core_peer, (x_peer, y_peer)),
    )

    def load(pair, kind, which):
        piece = 2 * pair + kind
        return pltpu.make_async_copy(deltas.at[:, c, :, :, columns(piece)], held.at[piece], load_sem.at[which])

    states = (
        pltpu.make_async_copy(master, mbuf, state_sem.at[0]),
        pltpu.make_async_copy(momentum, vbuf, state_sem.at[1]),
    )
    slot = (c * 2 + x) * 2 + y
    tok_load = pltpu.make_async_copy(tokens, raw, own_sem.at[2])
    tok_keep = pltpu.make_async_copy(cut.at[o * 2 + y], tokg.at[slot], own_sem.at[1])
    tok_group = [
        pltpu.make_async_remote_copy(
            src_ref=cut.at[share], dst_ref=tokg.at[slot], send_sem=gsend.at[0], recv_sem=grecv.at[0],
            device_id=peer, device_id_type=MESH,
        )
        for peer, share in group
    ]
    group_all = pltpu.make_async_remote_copy(
        src_ref=cut.at[pl.ds(0, count - 1)], dst_ref=tokg.at[pl.ds(0, count - 1)], send_sem=gsend.at[0],
        recv_sem=grecv.at[0], device_id=core_peer, device_id_type=MESH,
    )
    tok_own = pltpu.make_async_copy(tokg, tokf.at[f], own_sem.at[0])
    tok_along = [
        pltpu.make_async_remote_copy(
            src_ref=tokg, dst_ref=tokf.at[f], send_sem=fsend.at[0], recv_sem=frecv.at[0],
            device_id=peer, device_id_type=MESH,
        )
        for peer in along
    ]
    along_box = tokf.at[pl.ds(0, fsdp_count - 1)]
    along_all = pltpu.make_async_remote_copy(
        src_ref=along_box, dst_ref=along_box, send_sem=fsend.at[0], recv_sem=frecv.at[0],
        device_id=core_peer, device_id_type=MESH,
    )
    fresh_copy = pltpu.make_async_copy(mbuf, fresh_out, fresh_sem.at[0])

    pairs = pieces // 2

    def over(body, start=0, stop=pairs):
        def step(pair, carry):
            body(pair)
            return carry

        lax.fori_loop(start, stop, step, 0)

    rows = held.shape[3]
    step = rows // (HEAD * PACK) * PACK
    cuts = [pl.ds(h * step, step if h < HEAD - 1 else rows - h * step) for h in range(HEAD)] if step else [pl.ds(0, rows)]

    def held_wait(start, size, which):
        box = held.at[pl.ds(start, size)]
        pltpu.make_async_copy(box, box, load_sem.at[which]).wait()

    def fetch(pair):
        @pl.when(pair > 0)
        def _():
            for kind in range(2):
                load(pair, kind, 1).start()

    def first(pair):
        @pl.when(pair + AHEAD < pairs)
        def _():
            sums.go0(pair + AHEAD)

        @pl.when(pair == 1)
        def _():
            held_wait(2, pieces - 2, 1)

        @pl.when(pair > 0)
        def _():
            sums.go1(pair)

        @pl.when(pair >= LAG)
        def _():
            sums.go2(pair - LAG)

    tok_load.start()
    for kind in range(2):
        load(0, kind, 0).start()

    @pl.when(c == 0)
    def _():
        pl.semaphore_wait(barrier, 1 + 6 * corner)
        pl.semaphore_signal(core_sem, inc=1, device_id=core_peer, device_id_type=MESH)

    @pl.when(c == 1)
    def _():
        pl.semaphore_wait(core_sem, 1)

    sums.head0(cuts, head_sem)
    for pair in range(1, min(AHEAD, pairs)):
        sums.go0(pair)
    over(fetch)

    @pl.when(lead == 1)
    def _():
        for peer in along:
            pl.semaphore_signal(barrier, inc=1, device_id=peer, device_id_type=MESH)

    tok_load.wait()
    depth = cut.shape[2]
    cut[...] = jnp.zeros_like(cut)
    for g in range(count):
        cut[g, :token_rows] = f32(raw[...])[:, g * depth:(g + 1) * depth].astype(jnp.bfloat16)
    tok_keep.start()

    @pl.when((c == 1) & (corner == 0))
    def _():
        pl.semaphore_wait(barrier, 6)
        pl.semaphore_signal(plane_sem, inc=1, device_id=core_peer, device_id_type=MESH)

    @pl.when((c == 0) & (corner == 0))
    def _():
        pl.semaphore_wait(plane_sem, 1)

    for copy in tok_group:
        copy.start()
    held_wait(0, 2, 0)
    sums.head1(cuts, head_sem)
    lag = min(LAG, pairs)
    over(first, 0, lag)
    for copy in states:
        copy.start()
    tok_keep.wait()
    group_all.wait_recv()
    tok_own.start()

    @pl.when(lead == 1)
    def _():
        pl.semaphore_wait(barrier, len(along))
        for peer, _ in group:
            pl.semaphore_signal(all_sem, inc=1, device_id=peer, device_id_type=MESH)

    @pl.when(lead == 0)
    def _():
        pl.semaphore_wait(all_sem, 1)

    for copy in tok_along:
        copy.start()
    over(first, lag, pairs)
    tok_own.wait()
    along_all.wait_recv()
    for g in range(count):
        for k in range(fsdp_count):
            packed[g, pl.ds(k * token_rows, token_rows), :] = f32(tokf[k, g])[:token_rows]
    tok[...] = packed[...].astype(jnp.bfloat16).reshape(tok.shape)

    over(sums.go2, pairs - lag, pairs)
    for copy in states:
        copy.wait()

    def update(pair):
        sums.got(2, pair)
        for kind in range(2):
            piece = 2 * pair + kind
            at = columns(piece)
            average = sums.last(piece, kind) / count
            moment = decay_rate * vbuf[:, at] + average
            fresh = mbuf[:, at] - outer_rate * (average + decay_rate * moment)
            mbuf[:, at] = fresh
            product = jnp.dot(tok[...], fresh.astype(jnp.bfloat16), preferred_element_type=jnp.float32)
            product = product.astype(jnp.bfloat16).reshape((2, 2, 2) + hbuf.shape[:1] + (width,))
            part[0, piece] = product[0]
            part[1, piece] = product[1]
        prods.go0(pair)

        @pl.when(pair > 0)
        def _():
            prods.go1(pair - 1)

    over(update)
    prods.go1(pairs - 1)
    fresh_copy.start()
    over(prods.go2)

    def shown_copy(pair):
        at = pl.ds(pl.multiple_of(pair * 2 * width, LANES), 2 * width)
        return pltpu.make_async_copy(hbuf.at[:, at], shown_out.at[:, at], shown_sem.at[0])

    def finish(pair):
        prods.got(2, pair)
        for kind in range(2):
            piece = 2 * pair + kind
            v = prods.last(piece, kind)
            inner = 0.7978845608028654 * (v + 0.044715 * (v * v * v))
            hbuf[:, columns(piece)] = (0.5 * v * (1.0 + jnp.tanh(inner))).astype(jnp.bfloat16)
        shown_copy(pair).start()

    over(finish)
    sums.sent()
    prods.sent()
    group_all.wait_send()
    along_all.wait_send()
    fresh_copy.wait()
    pltpu.make_async_copy(hbuf, shown_out, shown_sem.at[0]).wait()


def fast_shards(pieces, deltas, master, momentum, tokens):
    fsdp_count = lax.axis_size("fsdp")
    count = lax.axis_size("outer") * lax.axis_size("rep")
    depth, wide = deltas.shape[1:]
    rows = depth // count
    width = wide // pieces
    token_rows = tokens.shape[1]
    padded = -(-token_rows // PACK) * PACK
    own_tokens = token_rows * fsdp_count
    blocks = deltas.reshape(2, 2, 2, rows, wide)
    half = jnp.bfloat16
    dma = pltpu.SemaphoreType.DMA
    regular = pltpu.SemaphoreType.REGULAR
    anywhere = pl.BlockSpec(memory_space=pl.ANY)
    new_master, hidden = pl.pallas_call(
        functools.partial(kernel, pieces, width, fsdp_count, count, token_rows),
        out_shape=(
            pltpu.VMEM((rows, wide), jnp.float32),
            pltpu.VMEM((own_tokens, wide), half),
        ),
        in_specs=[anywhere] * 4,
        out_specs=(anywhere, anywhere),
        scratch_shapes=[
            pltpu.VMEM((pieces, 2, 2, rows, width), half),
            pltpu.VMEM((pieces, 2, 2, rows, width), half),
            pltpu.VMEM((pieces, 2, rows, width), half),
            pltpu.VMEM((pieces, rows, width), half),
            pltpu.VMEM((2, pieces, 2, 2, own_tokens, width), half),
            pltpu.VMEM((pieces, 2, 2, own_tokens, width), half),
            pltpu.VMEM((pieces, 2, own_tokens, width), half),
            pltpu.VMEM((pieces, own_tokens, width), half),
            pltpu.VMEM((rows, wide), jnp.float32),
            pltpu.VMEM((own_tokens, wide), half),
            pltpu.VMEM((rows, wide), jnp.float32),
            pltpu.VMEM((token_rows, depth), half),
            pltpu.VMEM((count, padded, rows), half),
            pltpu.VMEM((count, padded, rows), half),
            pltpu.VMEM((fsdp_count, count, padded, rows), half),
            pltpu.VMEM((count, own_tokens, rows), jnp.float32),
            pltpu.VMEM((count * own_tokens, rows), half),
            dma((3,)), dma((3, pieces // 2)), dma((3,)), dma((3, pieces // 2)),
            dma((2,)), dma((2,)), dma((HEAD,)),
            dma((1,)), dma((1,)), dma((1,)), dma((1,)), dma((3,)),
            dma((1,)), dma((1,)),
            regular, regular, regular,
        ],
        compiler_params=pltpu.CompilerParams(
            collective_id=0, has_side_effects=True, vmem_limit_bytes=58 * 1024 * 1024
        ),
    )(blocks, master, momentum, tokens[0])
    parts = 8 if rows % 64 == 0 else 4 if rows % 32 == 0 else 1
    return pl.pallas_call(
        functools.partial(write_out, parts),
        out_shape=(
            jax.ShapeDtypeStruct((rows, wide), jnp.float32),
            jax.ShapeDtypeStruct((1, own_tokens, wide), half),
        ),
        in_specs=[pl.BlockSpec(memory_space=pltpu.VMEM)] * 2,
        out_specs=(anywhere, anywhere),
        scratch_shapes=[dma((parts + 1,))],
        compiler_params=pltpu.CompilerParams(vmem_limit_bytes=1024 * 1024),
    )(
        pltpu.with_memory_space_constraint(new_master, pltpu.VMEM),
        pltpu.with_memory_space_constraint(hidden, pltpu.VMEM),
    )


def write_out(parts, fresh, shown, new_master, hidden, sem):
    rows = fresh.shape[0] // parts
    copies = [
        pltpu.make_async_copy(fresh.at[pl.ds(k * rows, rows)], new_master.at[pl.ds(k * rows, rows)], sem.at[k])
        for k in range(parts)
    ]
    copies.append(pltpu.make_async_copy(shown, hidden.at[0], sem.at[parts]))
    for copy in copies:
        copy.start()
    for copy in copies:
        copy.wait()


def pieces_for(mesh, deltas):
    if mesh.shape["outer"] != 4 or mesh.shape["rep"] != 2:
        return None
    count = mesh.shape["outer"] * mesh.shape["rep"]
    wide = deltas.shape[2] // mesh.shape["fsdp"]
    if deltas.shape[1] % (count * PACK):
        return None
    for pieces in (18, 16, 12, 10, 8, 6, 4, 2):
        if wide % (pieces * LANES) == 0:
            return pieces
    return None


def solution(mesh):
    in_specs = (
        P(("outer", "rep"), None, "fsdp"),
        P(("outer", "rep"), "fsdp"),
        P(("outer", "rep"), "fsdp"),
        P(("outer", "rep"), "fsdp", None),
    )
    out_specs = (P(("outer", "rep"), "fsdp"), P(("outer", "rep"), None, "fsdp"))

    def run(deltas, master, momentum, tokens):
        pieces = pieces_for(mesh, deltas)
        shards = plain_shards if pieces is None else functools.partial(fast_shards, pieces)
        return jax.shard_map(shards, mesh=mesh, in_specs=in_specs, out_specs=out_specs, check_vma=False)(
            deltas, master, momentum, tokens
        )

    return run
```

```python
import functools

import jax
import jax.numpy as jnp
from jax import lax
from jax.experimental import pallas as pl
from jax.experimental.pallas import tpu as pltpu
from jax.sharding import PartitionSpec as P

outer_rate = 0.7
decay_rate = 0.9
LANES = 128
PACK = 16
AHEAD = 1
HEAD = 6
LAG = 6
MESH = pl.DeviceIdType.MESH


def plain_shards(deltas, master, momentum, tokens):
    outer_count = lax.axis_size("outer")
    rep_count = lax.axis_size("rep")
    terms = deltas[0].astype(jnp.float32)
    whole_tokens = lax.all_gather(tokens, "fsdp", axis=1, tiled=True)[0]
    summed = lax.psum_scatter(
        terms.astype(jnp.bfloat16), ("outer", "rep"), scatter_dimension=0, tiled=True
    ).astype(jnp.float32)
    average = summed / (outer_count * rep_count)
    moment = decay_rate * momentum + average
    new_master = master - outer_rate * (average + decay_rate * moment)
    weights = new_master.astype(jnp.bfloat16)
    product = jnp.dot(
        whole_tokens,
        lax.all_gather(weights, ("outer", "rep"), axis=0, tiled=True),
        preferred_element_type=jnp.float32,
    )
    hidden = jax.nn.gelu(product, approximate=True).astype(jnp.bfloat16)[None]
    return (new_master, hidden)


def f32(v):
    return v.astype(jnp.float32)


class Exchange:
    def __init__(self, given, held, r0, r1, r2, send, recv, at, peers):
        self.given, self.held = given, held
        self.r0, self.r1, self.r2 = r0, r1, r2
        self.send, self.recv = send, recv
        self.x, self.y = at
        self.core, self.peers = peers

    def copy(self, stage, src, dst, pair, peer):
        return pltpu.make_async_remote_copy(
            src_ref=src,
            dst_ref=dst,
            send_sem=self.send.at[stage],
            recv_sem=self.recv.at[stage, pair],
            device_id=peer,
            device_id_type=MESH,
        )

    def got(self, stage, pair):
        box = (self.r0, self.r1, self.r2)[stage].at[pl.ds(2 * pair, 2)]
        self.copy(stage, box, box, pair, self.core).wait_recv()

    def sent(self):
        for stage, box in enumerate((self.r0, self.r1, self.r2)):
            self.copy(stage, box, box, 0, self.core).wait_send()

    def spot2(self, kind):
        return (self.x, 1 - self.y) if kind == 0 else (1 - self.x, self.y)

    def go0(self, pair):
        for kind in range(2):
            piece = 2 * pair + kind
            self.copy(0, self.given(piece), self.r0.at[piece], pair, self.core).start()

    def forward1(self, pair, at):
        for kind in range(2):
            piece = 2 * pair + kind
            for k in range(2):
                a, b = (1 - self.x, k) if kind == 0 else (k, 1 - self.y)
                total = f32(self.held[piece, a, b, at]) + f32(self.r0[piece, a, b, at])
                self.held[piece, a, b, at] = total.astype(jnp.bfloat16)
            src = self.held.at[piece, 1 - self.x, :, at] if kind == 0 else self.held.at[piece, :, 1 - self.y, at]
            self.copy(1, src, self.r1.at[piece, :, at], pair, self.peers[kind]).start()

    def go1(self, pair):
        self.got(0, pair)
        self.forward1(pair, pl.ds(0, self.r0.shape[3]))

    def head0(self, cuts, sem):
        for h, at in enumerate(cuts):
            for kind in range(2):
                pltpu.make_async_remote_copy(
                    src_ref=self.given(kind).at[:, :, at], dst_ref=self.r0.at[kind, :, :, at],
                    send_sem=self.send.at[0], recv_sem=sem.at[h], device_id=self.core, device_id_type=MESH,
                ).start()

    def head1(self, cuts, sem):
        for h, at in enumerate(cuts):
            box = self.r0.at[pl.ds(0, 2), :, :, at]
            pltpu.make_async_remote_copy(
                src_ref=box, dst_ref=box, send_sem=self.send.at[0], recv_sem=sem.at[h],
                device_id=self.core, device_id_type=MESH,
            ).wait_recv()
            self.forward1(0, at)

    def go2(self, pair):
        self.got(1, pair)
        for kind in range(2):
            piece = 2 * pair + kind
            a, b = self.spot2(kind)
            total = f32(self.held[piece, a, b]) + f32(self.r0[piece, a, b])
            total = total + f32(self.r1[piece, b if kind == 0 else a])
            self.held[piece, a, b] = total.astype(jnp.bfloat16)
            self.copy(2, self.held.at[piece, a, b], self.r2.at[piece], pair, self.peers[1 - kind]).start()

    def last(self, piece, kind):
        total = f32(self.held[piece, self.x, self.y]) + f32(self.r0[piece, self.x, self.y])
        total = total + f32(self.r1[piece, self.y if kind == 0 else self.x])
        return total + f32(self.r2[piece])


def kernel(
    pieces, width, fsdp_count, count, token_rows,
    deltas, master, momentum, tokens, mbuf, hbuf,
    held, d0, d1, d2, part, p0, p1, p2, vbuf, raw, cut, tokg, tokf, packed, tok,
    dsend, drecv, psend, precv, load_sem, state_sem, head_sem,
    fsend, frecv, gsend, grecv, own_sem,
    core_sem, plane_sem, all_sem,
):
    o, y, f = lax.axis_index("outer"), lax.axis_index("rep"), lax.axis_index("fsdp")
    x, c = o // 2, o % 2
    core_peer = {"outer": x * 2 + 1 - c}
    x_peer = {"outer": (1 - x) * 2 + c}
    y_peer = {"rep": 1 - y}

    def flip(v, bit):
        return 1 - v if bit else v

    others = [(dc, dx, dy) for dc in range(2) for dx in range(2) for dy in range(2)][1:]
    group = [
        ({"outer": flip(x, dx) * 2 + flip(c, dc), "rep": flip(y, dy)},
         (flip(x, dx) * 2 + flip(c, dc)) * 2 + flip(y, dy))
        for dc, dx, dy in others
    ]
    along = [{"fsdp": (f + k) % fsdp_count} for k in range(1, fsdp_count)]

    corner = x * y
    lead = corner * c

    def counter(at_x, at_y):
        return {"outer": at_x * 2 + 1 - at_x * at_y, "rep": at_y}

    barrier = pltpu.get_barrier_semaphore()
    for at_x, at_y in ((1 - x, y), (x, 1 - y), (1 - x, 1 - y)):
        pl.semaphore_signal(barrier, inc=1, device_id=counter(at_x, at_y), device_id_type=MESH)

    @pl.when(c == 1)
    def _():
        pl.semaphore_signal(barrier, inc=1, device_id=core_peer, device_id_type=MESH)

    def columns(piece):
        return pl.ds(pl.multiple_of(piece * width, LANES), width)

    sums = Exchange(
        lambda piece: deltas.at[:, 1 - c, :, :, columns(piece)],
        held, d0, d1, d2, dsend, drecv, (x, y), (core_peer, (x_peer, y_peer)),
    )
    prods = Exchange(
        lambda piece: part.at[1 - c, piece],
        part.at[c], p0, p1, p2, psend, precv, (x, y), (core_peer, (x_peer, y_peer)),
    )

    def load(pair, kind, which):
        piece = 2 * pair + kind
        return pltpu.make_async_copy(deltas.at[:, c, :, :, columns(piece)], held.at[piece], load_sem.at[which])

    states = (
        pltpu.make_async_copy(master, mbuf, state_sem.at[0]),
        pltpu.make_async_copy(momentum, vbuf, state_sem.at[1]),
    )
    slot = (c * 2 + x) * 2 + y
    tok_load = pltpu.make_async_copy(tokens, raw, own_sem.at[2])
    tok_keep = pltpu.make_async_copy(cut.at[o * 2 + y], tokg.at[slot], own_sem.at[1])
    tok_group = [
        pltpu.make_async_remote_copy(
            src_ref=cut.at[share], dst_ref=tokg.at[slot], send_sem=gsend.at[0], recv_sem=grecv.at[0],
            device_id=peer, device_id_type=MESH,
        )
        for peer, share in group
    ]
    group_all = pltpu.make_async_remote_copy(
        src_ref=cut.at[pl.ds(0, count - 1)], dst_ref=tokg.at[pl.ds(0, count - 1)], send_sem=gsend.at[0],
        recv_sem=grecv.at[0], device_id=core_peer, device_id_type=MESH,
    )
    tok_own = pltpu.make_async_copy(tokg, tokf.at[f], own_sem.at[0])
    tok_along = [
        pltpu.make_async_remote_copy(
            src_ref=tokg, dst_ref=tokf.at[f], send_sem=fsend.at[0], recv_sem=frecv.at[0],
            device_id=peer, device_id_type=MESH,
        )
        for peer in along
    ]
    along_box = tokf.at[pl.ds(0, fsdp_count - 1)]
    along_all = pltpu.make_async_remote_copy(
        src_ref=along_box, dst_ref=along_box, send_sem=fsend.at[0], recv_sem=frecv.at[0],
        device_id=core_peer, device_id_type=MESH,
    )

    pairs = pieces // 2

    def over(body, start=0, stop=pairs):
        def step(pair, carry):
            body(pair)
            return carry

        lax.fori_loop(start, stop, step, 0)

    rows = held.shape[3]
    step = rows // (HEAD * PACK) * PACK
    cuts = [pl.ds(h * step, step if h < HEAD - 1 else rows - h * step) for h in range(HEAD)] if step else [pl.ds(0, rows)]

    def held_wait(start, size, which):
        box = held.at[pl.ds(start, size)]
        pltpu.make_async_copy(box, box, load_sem.at[which]).wait()

    def fetch(pair):
        @pl.when(pair > 0)
        def _():
            for kind in range(2):
                load(pair, kind, 1).start()

    def first(pair):
        @pl.when(pair + AHEAD < pairs)
        def _():
            sums.go0(pair + AHEAD)

        @pl.when(pair == 1)
        def _():
            held_wait(2, pieces - 2, 1)

        @pl.when(pair > 0)
        def _():
            sums.go1(pair)

        @pl.when(pair >= LAG)
        def _():
            sums.go2(pair - LAG)

    tok_load.start()
    for kind in range(2):
        load(0, kind, 0).start()

    @pl.when(c == 0)
    def _():
        pl.semaphore_wait(barrier, 1 + 6 * corner)
        pl.semaphore_signal(core_sem, inc=1, device_id=core_peer, device_id_type=MESH)

    @pl.when(c == 1)
    def _():
        pl.semaphore_wait(core_sem, 1)

    sums.head0(cuts, head_sem)
    for pair in range(1, min(AHEAD, pairs)):
        sums.go0(pair)
    over(fetch)

    @pl.when(lead == 1)
    def _():
        for peer in along:
            pl.semaphore_signal(barrier, inc=1, device_id=peer, device_id_type=MESH)

    tok_load.wait()
    depth = cut.shape[2]
    cut[...] = jnp.zeros_like(cut)
    for g in range(count):
        cut[g, :token_rows] = f32(raw[...])[:, g * depth:(g + 1) * depth].astype(jnp.bfloat16)
    tok_keep.start()

    @pl.when((c == 1) & (corner == 0))
    def _():
        pl.semaphore_wait(barrier, 6)
        pl.semaphore_signal(plane_sem, inc=1, device_id=core_peer, device_id_type=MESH)

    @pl.when((c == 0) & (corner == 0))
    def _():
        pl.semaphore_wait(plane_sem, 1)

    for copy in tok_group:
        copy.start()
    held_wait(0, 2, 0)
    sums.head1(cuts, head_sem)
    lag = min(LAG, pairs)
    over(first, 0, lag)
    for copy in states:
        copy.start()
    tok_keep.wait()
    group_all.wait_recv()
    tok_own.start()

    @pl.when(lead == 1)
    def _():
        pl.semaphore_wait(barrier, len(along))
        for peer, _ in group:
            pl.semaphore_signal(all_sem, inc=1, device_id=peer, device_id_type=MESH)

    @pl.when(lead == 0)
    def _():
        pl.semaphore_wait(all_sem, 1)

    for copy in tok_along:
        copy.start()
    over(first, lag, pairs)
    tok_own.wait()
    along_all.wait_recv()
    for g in range(count):
        for k in range(fsdp_count):
            packed[g, pl.ds(k * token_rows, token_rows), :] = f32(tokf[k, g])[:token_rows]
    tok[...] = packed[...].astype(jnp.bfloat16).reshape(tok.shape)

    over(sums.go2, pairs - lag, pairs)
    for copy in states:
        copy.wait()

    def update(pair):
        sums.got(2, pair)
        for kind in range(2):
            piece = 2 * pair + kind
            at = columns(piece)
            average = sums.last(piece, kind) / count
            moment = decay_rate * vbuf[:, at] + average
            fresh = mbuf[:, at] - outer_rate * (average + decay_rate * moment)
            mbuf[:, at] = fresh
            product = jnp.dot(tok[...], fresh.astype(jnp.bfloat16), preferred_element_type=jnp.float32)
            product = product.astype(jnp.bfloat16).reshape((2, 2, 2) + hbuf.shape[:1] + (width,))
            part[0, piece] = product[0]
            part[1, piece] = product[1]
        prods.go0(pair)

        @pl.when(pair > 0)
        def _():
            prods.go1(pair - 1)

    over(update)
    prods.go1(pairs - 1)
    over(prods.go2)

    def finish(pair):
        prods.got(2, pair)
        for kind in range(2):
            piece = 2 * pair + kind
            v = prods.last(piece, kind)
            inner = 0.7978845608028654 * (v + 0.044715 * (v * v * v))
            hbuf[:, columns(piece)] = (0.5 * v * (1.0 + jnp.tanh(inner))).astype(jnp.bfloat16)

    over(finish)
    sums.sent()
    prods.sent()
    group_all.wait_send()
    along_all.wait_send()


def fast_shards(pieces, deltas, master, momentum, tokens):
    fsdp_count = lax.axis_size("fsdp")
    count = lax.axis_size("outer") * lax.axis_size("rep")
    depth, wide = deltas.shape[1:]
    rows = depth // count
    width = wide // pieces
    token_rows = tokens.shape[1]
    padded = -(-token_rows // PACK) * PACK
    own_tokens = token_rows * fsdp_count
    blocks = deltas.reshape(2, 2, 2, rows, wide)
    half = jnp.bfloat16
    dma = pltpu.SemaphoreType.DMA
    regular = pltpu.SemaphoreType.REGULAR
    anywhere = pl.BlockSpec(memory_space=pl.ANY)
    new_master, hidden = pl.pallas_call(
        functools.partial(kernel, pieces, width, fsdp_count, count, token_rows),
        out_shape=(
            pltpu.VMEM((rows, wide), jnp.float32),
            pltpu.VMEM((own_tokens, wide), half),
        ),
        in_specs=[anywhere] * 4,
        out_specs=(pl.BlockSpec(memory_space=pltpu.VMEM),) * 2,
        scratch_shapes=[
            pltpu.VMEM((pieces, 2, 2, rows, width), half),
            pltpu.VMEM((pieces, 2, 2, rows, width), half),
            pltpu.VMEM((pieces, 2, rows, width), half),
            pltpu.VMEM((pieces, rows, width), half),
            pltpu.VMEM((2, pieces, 2, 2, own_tokens, width), half),
            pltpu.VMEM((pieces, 2, 2, own_tokens, width), half),
            pltpu.VMEM((pieces, 2, own_tokens, width), half),
            pltpu.VMEM((pieces, own_tokens, width), half),
            pltpu.VMEM((rows, wide), jnp.float32),
            pltpu.VMEM((token_rows, depth), half),
            pltpu.VMEM((count, padded, rows), half),
            pltpu.VMEM((count, padded, rows), half),
            pltpu.VMEM((fsdp_count, count, padded, rows), half),
            pltpu.VMEM((count, own_tokens, rows), jnp.float32),
            pltpu.VMEM((count * own_tokens, rows), half),
            dma((3,)), dma((3, pieces // 2)), dma((3,)), dma((3, pieces // 2)),
            dma((2,)), dma((2,)), dma((HEAD,)),
            dma((1,)), dma((1,)), dma((1,)), dma((1,)), dma((3,)),
            regular, regular, regular,
        ],
        compiler_params=pltpu.CompilerParams(
            collective_id=0, has_side_effects=True, vmem_limit_bytes=58 * 1024 * 1024
        ),
    )(blocks, master, momentum, tokens[0])
    parts = 8 if rows % 64 == 0 else 4 if rows % 32 == 0 else 1
    return pl.pallas_call(
        functools.partial(write_out, parts),
        out_shape=(
            jax.ShapeDtypeStruct((rows, wide), jnp.float32),
            jax.ShapeDtypeStruct((1, own_tokens, wide), half),
        ),
        in_specs=[pl.BlockSpec(memory_space=pltpu.VMEM)] * 2,
        out_specs=(anywhere, anywhere),
        scratch_shapes=[dma((parts + 1,))],
        compiler_params=pltpu.CompilerParams(vmem_limit_bytes=1024 * 1024),
    )(
        pltpu.with_memory_space_constraint(new_master, pltpu.VMEM),
        pltpu.with_memory_space_constraint(hidden, pltpu.VMEM),
    )


def write_out(parts, fresh, shown, new_master, hidden, sem):
    rows = fresh.shape[0] // parts
    copies = [
        pltpu.make_async_copy(fresh.at[pl.ds(k * rows, rows)], new_master.at[pl.ds(k * rows, rows)], sem.at[k])
        for k in range(parts)
    ]
    copies.append(pltpu.make_async_copy(shown, hidden.at[0], sem.at[parts]))
    for copy in copies:
        copy.start()
    for copy in copies:
        copy.wait()


def pieces_for(mesh, deltas):
    if mesh.shape["outer"] != 4 or mesh.shape["rep"] != 2:
        return None
    count = mesh.shape["outer"] * mesh.shape["rep"]
    wide = deltas.shape[2] // mesh.shape["fsdp"]
    if deltas.shape[1] % (count * PACK):
        return None
    for pieces in (12, 18, 16, 10, 8, 6, 4, 2):
        if wide % (pieces * LANES) == 0:
            return pieces
    return None


def solution(mesh):
    in_specs = (
        P(("outer", "rep"), None, "fsdp"),
        P(("outer", "rep"), "fsdp"),
        P(("outer", "rep"), "fsdp"),
        P(("outer", "rep"), "fsdp", None),
    )
    out_specs = (P(("outer", "rep"), "fsdp"), P(("outer", "rep"), None, "fsdp"))

    def run(deltas, master, momentum, tokens):
        pieces = pieces_for(mesh, deltas)
        shards = plain_shards if pieces is None else functools.partial(fast_shards, pieces)
        return jax.shard_map(shards, mesh=mesh, in_specs=in_specs, out_specs=out_specs, check_vma=False)(
            deltas, master, momentum, tokens
        )

    return run
```
